128 devices in a mesh: slab: 64 (over z, y, x), tile: 2 (over core).
Axes of the slice: x: 4, y: 4, z: 4, core: 2. Of those that a mesh axis runs over, the one named last changes fastest.
Arguments:
- samples: float32 [64, 256, 32, 256], P('slab', None, 'tile'), may hold values from -6 to 6
- counts: int32 [64, 256, 32], P('slab', None, 'tile'), may hold values from 1 to 4
- w_in: float32 [64, 64, 256], P('slab'), may hold values from -0.75 to 0.75
- b_in: float32 [64, 256], P('slab'), may hold values from -3 to 3
- w_color: float32 [64, 256, 128], P('slab'), may hold values from -0.375 to 0.375
- b_color: float32 [64, 128], P('slab'), may hold values from -3 to 3
- w_density: float32 [64, 256], P('slab'), may hold values from -0.375 to 0.375
- b_density: float32 [64], P('slab'), may hold values from -1 to 1
- conv_a: bfloat16 [3, 3, 128, 128], replicated, may hold values from -0.1875 to 0.1875
- bias_a: float32 [128], replicated, may hold values from -3 to 3
- conv_b: bfloat16 [3, 3, 128, 128], replicated, may hold values from -0.1875 to 0.1875
- bias_b: float32 [128], replicated, may hold values from -3 to 3
Outputs:
- decoded: bfloat16 [256, 32, 128], P('slab', 'tile')
- front: float32 [64, 256, 32], P('slab', None, 'tile')
The draws below stay inside these ranges and needn't reach their ends.
All inputs are finite; a program needn't handle non-finite values.
Results may differ from the reference program's by a relative error of at most 0.006.
Values may be sent and summed in bfloat16 or wider, within the bound.
No kernel may reach another device: no remote copies, remote signals or barrier semaphores. Data moves between devices by JAX's collectives and lax.ppermute only.
A program may use at most 128 MiB of HBM per device.

```python
import jax
import jax.numpy as jnp
from jax import lax

F = 64
HID = 256
C = 128
K = 4
STRIP = 4
SLABS = 64
HEIGHT = 256
WIDTH = 32


def place_ends(array, stream_key, least, largest):
    longest = array.shape.index(max(array.shape))
    spots = []
    for shift in (0, 1):
        where = [jax.random.randint(jax.random.fold_in(stream_key, axis), (), 0, length) for axis, length in enumerate(array.shape)]
        where[longest] = (where[longest] + shift) % array.shape[longest]
        spots.append(tuple(where))
    return array.at[spots[0]].set(least).at[spots[1]].set(largest)


def steps_of(own_key, dims, cuts, smallest, top_value):
    def one(axis_at, shards_of):
        steps = jax.random.uniform(jax.random.fold_in(jax.random.fold_in(own_key, 6), axis_at), (shards_of,), jnp.float32, smallest / len(cuts), top_value / len(cuts))
        return jnp.repeat(jnp.exp(steps), dims[axis_at] // shards_of).reshape((-1,) + (1,) * (len(dims) - axis_at - 1))

    gain = one(*cuts[0])
    for cut in cuts[1:]:
        gain = gain * one(*cut)
    return gain


def gaussian(stream_key, dims, spread, reach, cuts=(), held_as=jnp.bfloat16):
    factor_of = steps_of(stream_key, dims, cuts, -0.22, 0.18) if cuts else 1.0
    entries = jax.random.normal(stream_key, dims, jnp.float32) * spread * factor_of
    return jnp.minimum(jnp.maximum(entries, -reach), reach).astype(held_as)


def setup_inputs(seed: int = 0) -> dict:
    arg_keys = jax.random.split(jax.random.key(seed), 13)
    return {
        "samples": gaussian(arg_keys[0], (SLABS, HEIGHT, WIDTH, K * F), 1.0, 6.0, ((0, 64), (2, 2)), jnp.float32),
        "counts": place_ends(jax.random.randint(arg_keys[1], (SLABS, HEIGHT, WIDTH), 1, K + 1), jax.random.fold_in(arg_keys[1], 1), 1, K).astype(jnp.int32),
        "w_in": gaussian(arg_keys[2], (SLABS, F, HID), F ** -0.5, 0.75, ((0, 64),), jnp.float32),
        "b_in": gaussian(arg_keys[3], (SLABS, HID), 0.5, 3.0, ((0, 64),), jnp.float32),
        "w_color": gaussian(arg_keys[4], (SLABS, HID, C), HID ** -0.5, 0.375, ((0, 64),), jnp.float32),
        "b_color": gaussian(arg_keys[5], (SLABS, C), 0.5, 3.0, ((0, 64),), jnp.float32),
        "w_density": gaussian(arg_keys[6], (SLABS, HID), HID ** -0.5, 0.375, ((0, 64),), jnp.float32),
        "b_density": jnp.clip(jax.random.uniform(arg_keys[7], (SLABS,), jnp.float32, -1.0, 1.0) * steps_of(arg_keys[7], (SLABS,), ((0, 64),), -0.4, 0.0), -1.0, 1.0),
        "conv_a": gaussian(arg_keys[8], (3, 3, C, C), (9 * C) ** -0.5, 0.1875),
        "bias_a": gaussian(arg_keys[9], (C,), 0.5, 3.0, (), jnp.float32),
        "conv_b": gaussian(arg_keys[10], (3, 3, C, C), (9 * C) ** -0.5, 0.1875),
        "bias_b": gaussian(arg_keys[11], (C,), 0.5, 3.0, (), jnp.float32),
    }


def hidden_units(inputs, w_in, b_in):
    shaped = inputs.reshape(inputs.shape[:-1] + (K, F))
    return jax.nn.relu(jnp.einsum('rwkf,fh->rwkh', shaped, w_in, precision=lax.Precision.HIGHEST) + b_in)


def densities(hidden_act, w_density, b_density, live_count):
    before = jnp.einsum('rwkh,h->rwk', hidden_act, w_density, precision=lax.Precision.HIGHEST) + b_density
    slots = lax.broadcasted_iota(jnp.int32, before.shape, 2)
    return jnp.where(slots < live_count[..., None], jax.nn.softplus(before), 0.0)


def sample_weights(density, front, total):
    scaled = density / total[..., None]
    earlier = jnp.cumsum(scaled, axis=2) - scaled
    return jnp.exp(-front[..., None] - earlier) * (1.0 - jnp.exp(-scaled))


def partial_image(hidden_act, weight, w_color, b_color):
    color = jnp.einsum('rwkh,hc->rwkc', hidden_act, w_color, precision=lax.Precision.HIGHEST) + b_color
    return jnp.einsum('rwk,rwkc->rwc', weight, color, precision=lax.Precision.HIGHEST)


def convolve(image, kernel):
    result = lax.conv_general_dilated(image.astype(jnp.float32)[None], kernel.astype(jnp.float32), (1, 1), 'SAME',
                                      dimension_numbers=('NHWC', 'HWIO', 'NHWC'), precision=lax.Precision.HIGHEST)
    return result[0]


def reference(samples, counts, w_in, b_in, w_color, b_color, w_density, b_density, conv_a, bias_a, conv_b, bias_b):
    blocks = HEIGHT // STRIP

    def slab_density(packed):
        inputs, live, first_w, first_b, dens_w, dens_b = packed

        def per_block(pair):
            return densities(hidden_units(pair[0], first_w, first_b), dens_w, dens_b, pair[1])

        pieces = lax.map(per_block, (inputs.reshape(blocks, STRIP, WIDTH, K * F), live.reshape(blocks, STRIP, WIDTH)))
        return pieces.reshape(HEIGHT, WIDTH, K)

    density = lax.map(slab_density, (samples, counts, w_in, b_in, w_density, b_density))
    depth = jnp.sum(density, axis=3)
    total = jnp.sum(depth, axis=0)
    prefix = jnp.cumsum(depth, axis=0) - depth
    front = prefix / total

    def add_slab(image, packed):
        inputs, dens, ahead, first_w, first_b, col_w, col_b = packed
        weight = sample_weights(dens, ahead, total)

        def per_block(pair):
            return partial_image(hidden_units(pair[0], first_w, first_b), pair[1], col_w, col_b)

        part = lax.map(per_block, (inputs.reshape(blocks, STRIP, WIDTH, K * F), weight.reshape(blocks, STRIP, WIDTH, K)))
        return image + part.reshape(HEIGHT, WIDTH, C), None

    start_image = jnp.zeros((HEIGHT, WIDTH, C), jnp.float32)
    image, _ = lax.scan(add_slab, start_image, (samples, density, front, w_in, b_in, w_color, b_color))
    image = image.astype(jnp.bfloat16)
    hidden_map = jax.nn.relu(convolve(image, conv_a) + bias_a).astype(jnp.bfloat16)
    decoded = (convolve(hidden_map, conv_b) + bias_b).astype(jnp.bfloat16)
    return (decoded, front)
```

```python
import jax
import jax.numpy as jnp
from jax import lax
from jax.experimental import pallas as pl
from jax.experimental.pallas import tpu as pltpu
from jax.sharding import PartitionSpec as P

F = 64
HID = 256
C = 128
K = 4
SLABS = 64
ROWS = 256
COLS = 16
RAYS = ROWS * COLS
LANES = 128
GROUPS = RAYS // LANES
BLOCK = 512
PER = BLOCK // LANES
STRIP = 4
BF = jnp.bfloat16
F32 = jnp.float32

NT = (((1,), (1,)), ((), ()))


def column(row, lanes):
    return jnp.broadcast_to(row, (lanes, row.shape[1])).T


def dense_kernel(x, counts, w_in, b_in, w_color, w_density, b_density,
                 color, density, depth, w_s, b_s, d_s, c_s, logit):
    step = pl.program_id(0)

    @pl.when(step == 0)
    def _():
        turned = w_in[0].T.astype(BF)
        w_s[...] = jnp.zeros_like(w_s)
        for k in range(K):
            w_s[k * HID:(k + 1) * HID, k * F:(k + 1) * F] = turned
        b_s[...] = column(b_in[...], LANES)
        d_s[...] = column(w_density[...], LANES)
        c_s[...] = w_color[0].T.astype(BF)

    rays = x[...].astype(BF)
    bias = jnp.concatenate([b_s[...]] * PER, axis=1)
    head = jnp.concatenate([d_s[...]] * PER, axis=1)
    for k in range(K):
        hidden = lax.dot_general(w_s[k * HID:(k + 1) * HID, :], rays, NT, preferred_element_type=F32)
        hidden = jnp.maximum(hidden + bias, 0.0)
        before = jnp.sum(hidden * head, axis=0, keepdims=True)
        for g in range(PER):
            logit[k, pl.ds(step * PER + g, 1), :] = before[:, g * LANES:(g + 1) * LANES]
        made = jnp.dot(c_s[...], hidden.astype(BF), preferred_element_type=F32)
        color[k] = made.astype(BF)

    @pl.when(step == pl.num_programs(0) - 1)
    def _():
        live = jnp.concatenate(
            [counts[0, pl.ds(a, GROUPS, stride=8), :] for a in range(8)], axis=1
        )
        total = jnp.zeros((GROUPS, LANES), F32)
        for k in range(K):
            pre = logit[k] + b_density[0]
            soft = jnp.maximum(pre, 0.0) + jnp.log1p(jnp.exp(-jnp.abs(pre)))
            soft = jnp.where(live > k, soft, 0.0)
            density[k] = soft
            total = total + soft
        depth[...] = jnp.broadcast_to(total.astype(BF)[None], depth.shape)


def weigh_kernel(depths, density, color, b_color, image, front, w_s, b_s):
    step = pl.program_id(0)

    @pl.when(step == 0)
    def _():
        place = lax.axis_index("slab")
        b_s[...] = column(b_color[...], LANES)

        def add(turn, state):
            total, ahead = state
            one = depths[turn].astype(F32)
            return total + one, ahead + jnp.where(turn < place, one, 0.0)

        zero = jnp.zeros((GROUPS, LANES), F32)
        total, ahead = lax.fori_loop(0, SLABS, add, (zero, zero), unroll=8)
        ahead = ahead / total
        for a in range(8):
            front[0, pl.ds(a, GROUPS, stride=8), :] = ahead[:, a * COLS:(a + 1) * COLS]
        passed = ahead
        for k in range(K):
            scaled = density[k] / total
            w_s[k] = jnp.exp(-passed) * (1.0 - jnp.exp(-scaled))
            passed = passed + scaled

    for g in range(PER):
        at = pl.ds(step * PER + g, 1)
        weights = [w_s[k, at, :] for k in range(K)]
        part = b_s[...] * (weights[0] + weights[1] + weights[2] + weights[3])
        for k in range(K):
            part = part + color[k, :, g * LANES:(g + 1) * LANES].astype(F32) * weights[k]
        image[g * LANES:(g + 1) * LANES, :] = part.T.astype(BF)


def sum_kernel(parts, strip, top, bottom):
    total = jnp.zeros((STRIP * COLS, C), F32)

    def add(turn, state):
        return state + parts[turn].astype(F32)

    total = lax.fori_loop(0, SLABS, add, total, unroll=8).astype(BF)
    strip[...] = total
    top[...] = total[:2 * COLS]
    bottom[...] = total[2 * COLS:]


PITCH = 32
EDGE = 8


def taps(field, rows):
    flat = field.reshape(-1, C)
    span = flat.shape[0]
    shifted = [pltpu.roll(flat, 1, 0).astype(BF), flat.astype(BF), pltpu.roll(flat, span - 1, 0).astype(BF)]
    return jnp.concatenate(
        [s[PITCH * r:PITCH * (r + rows)] for r in range(3) for s in shifted], axis=1
    )


def decode_kernel(strip, above, below, strip_p, above_p, below_p, conv_a, bias_a, conv_b, bias_b, out, patch):
    place = lax.axis_index("slab")
    tile = lax.axis_index("tile")
    first = place == 0
    last = place == SLABS - 1

    def whole(up, mid, down):
        up = jnp.where(first, 0.0, up[...].astype(F32))
        down = jnp.where(last, 0.0, down[...].astype(F32))
        return jnp.concatenate([up, mid[...].astype(F32), down], axis=0).reshape(STRIP + 4, COLS, C)

    own = whole(above, strip, below)
    other = whole(above_p, strip_p, below_p)
    patch[...] = jnp.zeros_like(patch)
    patch[:, EDGE:EDGE + COLS, :] = own
    patch[:, EDGE - 2:EDGE, :] = jnp.where(tile == 0, 0.0, other[:, COLS - 2:, :])
    patch[:, EDGE + COLS:EDGE + COLS + 2, :] = jnp.where(tile == 0, other[:, :2, :], 0.0)
    rows = STRIP + 2
    made = jnp.dot(taps(patch[...], rows), conv_a[...].reshape(9 * C, C), preferred_element_type=F32)
    made = jnp.maximum(made + bias_a[...], 0.0).astype(BF).astype(F32).reshape(rows, PITCH, C)
    row = lax.broadcasted_iota(jnp.int32, made.shape, 0) + (place * STRIP - 1)
    col = lax.broadcasted_iota(jnp.int32, made.shape, 1) + (tile * COLS - EDGE)
    inside = (row >= 0) & (row < ROWS) & (col >= 0) & (col < 2 * COLS)
    made = jnp.where(inside, made, 0.0)
    done = jnp.dot(taps(made, STRIP), conv_b[...].reshape(9 * C, C), preferred_element_type=F32) + bias_b[...]
    out[...] = done.reshape(STRIP, PITCH, C)[:, EDGE:EDGE + COLS, :].astype(BF)


def full(*shape):
    return pl.BlockSpec(shape, lambda i: (0,) * len(shape))


def body(samples, counts, w_in, b_in, w_color, b_color, w_density, b_density, conv_a, bias_a, conv_b, bias_b):
    vmem = pl.BlockSpec(memory_space=pltpu.VMEM)
    steps = RAYS // BLOCK
    color, density, depth = pl.pallas_call(
        dense_kernel,
        grid=(steps,),
        in_specs=[
            pl.BlockSpec((BLOCK, K * F), lambda i: (i, 0)),
            full(1, ROWS, COLS),
            full(1, F, HID),
            full(1, HID),
            full(1, HID, C),
            full(1, HID),
            pl.BlockSpec(memory_space=pltpu.SMEM),
        ],
        out_specs=[
            pl.BlockSpec((K, C, BLOCK), lambda i: (0, 0, i)),
            full(K, GROUPS, LANES),
            full(SLABS, GROUPS, LANES),
        ],
        out_shape=[
            jax.ShapeDtypeStruct((K, C, RAYS), BF),
            jax.ShapeDtypeStruct((K, GROUPS, LANES), F32),
            jax.ShapeDtypeStruct((SLABS, GROUPS, LANES), BF),
        ],
        scratch_shapes=[
            pltpu.VMEM((K * HID, K * F), BF),
            pltpu.VMEM((HID, LANES), F32),
            pltpu.VMEM((HID, LANES), F32),
            pltpu.VMEM((C, HID), BF),
            pltpu.VMEM((K, GROUPS, LANES), F32),
        ],
        name="dense",
    )(samples.reshape(RAYS, K * F), counts, w_in, b_in, w_color, w_density, b_density)

    depths = lax.all_to_all(depth, "slab", 0, 0, tiled=True)

    image, front = pl.pallas_call(
        weigh_kernel,
        grid=(steps,),
        in_specs=[
            full(SLABS, GROUPS, LANES),
            full(K, GROUPS, LANES),
            pl.BlockSpec((K, C, BLOCK), lambda i: (0, 0, i)),
            full(1, C),
        ],
        out_specs=[
            pl.BlockSpec((BLOCK, C), lambda i: (i, 0)),
            full(1, ROWS, COLS),
        ],
        out_shape=[
            jax.ShapeDtypeStruct((RAYS, C), BF),
            jax.ShapeDtypeStruct((1, ROWS, COLS), F32),
        ],
        scratch_shapes=[
            pltpu.VMEM((K, GROUPS, LANES), F32),
            pltpu.VMEM((C, LANES), F32),
        ],
        name="weigh",
    )(depths, density, color, b_color)

    parts = lax.all_to_all(image.reshape(SLABS, STRIP * COLS, C), "slab", 0, 0, tiled=True)

    strip, top, bottom = pl.pallas_call(
        sum_kernel,
        in_specs=[vmem],
        out_specs=[vmem] * 3,
        out_shape=[
            jax.ShapeDtypeStruct((STRIP * COLS, C), BF),
            jax.ShapeDtypeStruct((2 * COLS, C), BF),
            jax.ShapeDtypeStruct((2 * COLS, C), BF),
        ],
        name="gathered",
    )(parts)

    onward = [(i, (i + 1) % SLABS) for i in range(SLABS)]
    back = [(j, i) for i, j in onward]
    swap = [(0, 1), (1, 0)]
    above = lax.ppermute(bottom, "slab", onward)
    below = lax.ppermute(top, "slab", back)
    strip_p = lax.ppermute(strip, "tile", swap)
    above_p = lax.ppermute(above, "tile", swap)
    below_p = lax.ppermute(below, "tile", swap)

    decoded = pl.pallas_call(
        decode_kernel,
        in_specs=[vmem] * 10,
        out_specs=vmem,
        out_shape=jax.ShapeDtypeStruct((STRIP, COLS, C), BF),
        scratch_shapes=[pltpu.VMEM((STRIP + 4, PITCH, C), F32)],
        name="decode",
    )(strip, above, below, strip_p, above_p, below_p, conv_a, bias_a.reshape(1, C), conv_b, bias_b.reshape(1, C))
    return decoded, front


def solution(mesh):
    in_specs = (
        P("slab", None, "tile", None),
        P("slab", None, "tile"),
        P("slab", None, None),
        P("slab", None),
        P("slab", None, None),
        P("slab", None),
        P("slab", None),
        P("slab"),
        P(),
        P(),
        P(),
        P(),
    )
    out_specs = (P("slab", "tile", None), P("slab", None, "tile"))
    return jax.shard_map(body, mesh=mesh, in_specs=in_specs, out_specs=out_specs, check_vma=False)
```

```python
import jax
import jax.numpy as jnp
from jax import lax
from jax.experimental import pallas as pl
from jax.experimental.pallas import tpu as pltpu
from jax.sharding import PartitionSpec as P

F = 64
HID = 256
C = 128
K = 4
SLABS = 64
ROWS = 256
COLS = 16
RAYS = ROWS * COLS
LANES = 128
GROUPS = RAYS // LANES
BLOCK = 512
PER = BLOCK // LANES
STEPS = RAYS // BLOCK
HEAD = C + 16
STRIP = 4
BF = jnp.bfloat16
F32 = jnp.float32

NT = (((1,), (1,)), ((), ()))


def column(row, lanes):
    return jnp.broadcast_to(row, (lanes, row.shape[1])).T


def dense_kernel(samples, counts, w_in, b_in, w_color, w_density, b_density,
                 color, density, depth, x, w_s, b_s, c_s, logit, turn_s, sems):
    def fetch(step):
        return pltpu.make_async_copy(samples.at[pl.ds(step * BLOCK, BLOCK), :], x.at[step], sems.at[step])

    for step in range(STEPS):
        fetch(step).start()

    turned = w_in[0].T.astype(BF)
    w_s[...] = jnp.zeros_like(w_s)
    for k in range(K):
        w_s[k * HID:(k + 1) * HID, k * F:(k + 1) * F] = turned
    b_s[...] = column(b_in[...], LANES)
    c_s[:C, :] = w_color[0].T.astype(BF)
    head = w_density[...]
    coarse = head.astype(BF)
    fine = (head - coarse.astype(F32)).astype(BF)
    place = lax.broadcasted_iota(jnp.int32, (HEAD - C, HID), 0)
    c_s[C:, :] = jnp.where(
        place == 0, coarse.astype(F32), jnp.where(place == 1, fine.astype(F32), 0.0)
    ).astype(BF)

    def one(step, _):
        fetch(step).wait()
        rays = x[step].astype(BF)
        bias = jnp.concatenate([b_s[...]] * PER, axis=1)

        def first(k):
            return lax.dot_general(w_s[k * HID:(k + 1) * HID, :], rays, NT, preferred_element_type=F32)

        hidden = first(0)
        for k in range(K):
            ahead = first(k + 1) if k + 1 < K else None
            lit = jnp.maximum((hidden + bias).astype(BF), jnp.zeros((), BF))
            made = jnp.dot(c_s[...], lit, preferred_element_type=F32)
            color[k, :, pl.ds(step * BLOCK, BLOCK)] = made[:C].astype(BF)
            before = made[C:C + 1] + made[C + 1:C + 2]
            for g in range(PER):
                logit[k, pl.ds(step * PER + g, 1), :] = before[:, g * LANES:(g + 1) * LANES]
            hidden = ahead
        return 0

    lax.fori_loop(0, STEPS, one, 0)

    turn_s[...] = counts[0].astype(F32).T
    live = jnp.concatenate([turn_s[pl.ds(a, GROUPS, stride=8), :] for a in range(8)], axis=1)
    total = jnp.zeros((GROUPS, LANES), F32)
    for k in range(K):
        pre = logit[k] + b_density[0]
        soft = jnp.maximum(pre, 0.0) + jnp.log1p(jnp.exp(-jnp.abs(pre)))
        soft = jnp.where(live > k, soft, 0.0)
        density[k] = soft
        total = total + soft
    depth[...] = jnp.broadcast_to(total.astype(BF)[None], depth.shape)


def weigh_kernel(depths, density, color, b_color, image, front, w_s, b_s, turn_s):
    place = lax.axis_index("slab")
    b_s[...] = column(b_color[...], LANES)

    def add(turn, state):
        total, ahead = state
        one = depths[turn].astype(F32)
        return total + one, ahead + jnp.where(turn < place, one, 0.0)

    zero = jnp.zeros((GROUPS, LANES), F32)
    total, ahead = lax.fori_loop(0, SLABS, add, (zero, zero), unroll=8)
    ahead = ahead / total
    for a in range(8):
        turn_s[pl.ds(a, GROUPS, stride=8), :] = ahead[:, a * COLS:(a + 1) * COLS]
    front[0] = turn_s[...].T
    passed = ahead
    for k in range(K):
        scaled = density[k] / total
        w_s[k] = jnp.exp(-passed) * (1.0 - jnp.exp(-scaled))
        passed = passed + scaled

    def one(step, _):
        for g in range(PER):
            at = pl.ds(step * PER + g, 1)
            lanes = pl.ds((step * PER + g) * LANES, LANES)
            weights = [w_s[k, at, :] for k in range(K)]
            part = b_s[...] * (weights[0] + weights[1] + weights[2] + weights[3])
            for k in range(K):
                part = part + color[k, :, lanes].astype(F32) * weights[k]
            image[lanes, :] = part.T.astype(BF)
        return 0

    lax.fori_loop(0, STEPS, one, 0)


def sum_kernel(parts, strip, top, bottom):
    total = jnp.zeros((STRIP * COLS, C), F32)

    def add(turn, state):
        return state + parts[turn].astype(F32)

    total = lax.fori_loop(0, SLABS, add, total, unroll=8).astype(BF)
    strip[...] = total
    top[...] = total[:2 * COLS]
    bottom[...] = total[2 * COLS:]


PITCH = 32
EDGE = 8


def taps(field, rows):
    flat = field.reshape(-1, C)
    span = flat.shape[0]
    shifted = [pltpu.roll(flat, 1, 0).astype(BF), flat.astype(BF), pltpu.roll(flat, span - 1, 0).astype(BF)]
    return jnp.concatenate(
        [s[PITCH * r:PITCH * (r + rows)] for r in range(3) for s in shifted], axis=1
    )


def decode_kernel(strip, above, below, strip_p, above_p, below_p, conv_a, bias_a, conv_b, bias_b, out, patch):
    place = lax.axis_index("slab")
    tile = lax.axis_index("tile")
    first = place == 0
    last = place == SLABS - 1

    def whole(up, mid, down):
        up = jnp.where(first, 0.0, up[...].astype(F32))
        down = jnp.where(last, 0.0, down[...].astype(F32))
        return jnp.concatenate([up, mid[...].astype(F32), down], axis=0).reshape(STRIP + 4, COLS, C)

    own = whole(above, strip, below)
    other = whole(above_p, strip_p, below_p)
    patch[...] = jnp.zeros_like(patch)
    patch[:, EDGE:EDGE + COLS, :] = own
    patch[:, EDGE - 2:EDGE, :] = jnp.where(tile == 0, 0.0, other[:, COLS - 2:, :])
    patch[:, EDGE + COLS:EDGE + COLS + 2, :] = jnp.where(tile == 0, other[:, :2, :], 0.0)
    rows = STRIP + 2
    made = jnp.dot(taps(patch[...], rows), conv_a[...].reshape(9 * C, C), preferred_element_type=F32)
    made = jnp.maximum(made + bias_a[...], 0.0).astype(BF).astype(F32).reshape(rows, PITCH, C)
    row = lax.broadcasted_iota(jnp.int32, made.shape, 0) + (place * STRIP - 1)
    col = lax.broadcasted_iota(jnp.int32, made.shape, 1) + (tile * COLS - EDGE)
    inside = (row >= 0) & (row < ROWS) & (col >= 0) & (col < 2 * COLS)
    made = jnp.where(inside, made, 0.0)
    done = jnp.dot(taps(made, STRIP), conv_b[...].reshape(9 * C, C), preferred_element_type=F32) + bias_b[...]
    out[...] = done.reshape(STRIP, PITCH, C)[:, EDGE:EDGE + COLS, :].astype(BF)


def call(kernel, name, out, scratch=(), spaces=(), limit=4, given=0):
    vmem = pl.BlockSpec(memory_space=pltpu.VMEM)
    return pl.pallas_call(
        kernel,
        in_specs=[pl.BlockSpec(memory_space=dict(spaces).get(i, pltpu.VMEM)) for i in range(given)],
        out_specs=[vmem] * len(out),
        out_shape=out,
        scratch_shapes=list(scratch),
        compiler_params=pltpu.CompilerParams(vmem_limit_bytes=limit << 20),
        name=name,
    )


def body(samples, counts, w_in, b_in, w_color, b_color, w_density, b_density, conv_a, bias_a, conv_b, bias_b):
    shape = jax.ShapeDtypeStruct
    color, density, depth = call(
        dense_kernel,
        "dense",
        [
            shape((K, C, RAYS), BF),
            shape((K, GROUPS, LANES), F32),
            shape((SLABS, GROUPS, LANES), BF),
        ],
        [
            pltpu.VMEM((STEPS, BLOCK, K * F), F32),
            pltpu.VMEM((K * HID, K * F), BF),
            pltpu.VMEM((HID, LANES), F32),
            pltpu.VMEM((HEAD, HID), BF),
            pltpu.VMEM((K, GROUPS, LANES), F32),
            pltpu.VMEM((ROWS, COLS), F32),
            pltpu.SemaphoreType.DMA((STEPS,)),
        ],
        {0: pltpu.HBM, 6: pltpu.SMEM},
        16,
        7,
    )(pltpu.with_memory_space_constraint(samples.reshape(RAYS, K * F), pltpu.HBM), counts.transpose(0, 2, 1), w_in, b_in, w_color, w_density, b_density)

    depths = lax.all_to_all(depth, "slab", 0, 0, tiled=True)

    image, front = call(
        weigh_kernel,
        "weigh",
        [shape((RAYS, C), BF), shape((1, COLS, ROWS), F32)],
        [
            pltpu.VMEM((K, GROUPS, LANES), F32),
            pltpu.VMEM((C, LANES), F32),
            pltpu.VMEM((ROWS, COLS), F32),
        ],
        given=4,
        limit=16,
    )(depths, density, color, b_color)
    front = front.transpose(0, 2, 1)

    parts = lax.all_to_all(image.reshape(SLABS, STRIP * COLS, C), "slab", 0, 0, tiled=True)

    strip, top, bottom = call(
        sum_kernel,
        "gathered",
        [shape((STRIP * COLS, C), BF), shape((2 * COLS, C), BF), shape((2 * COLS, C), BF)],
        given=1,
        limit=8,
    )(parts)

    onward = [(i, (i + 1) % SLABS) for i in range(SLABS)]
    back = [(j, i) for i, j in onward]
    swap = [(0, 1), (1, 0)]
    above = lax.ppermute(bottom, "slab", onward)
    below = lax.ppermute(top, "slab", back)
    strip_p = lax.ppermute(strip, "tile", swap)
    above_p = lax.ppermute(above, "tile", swap)
    below_p = lax.ppermute(below, "tile", swap)

    (decoded,) = call(
        decode_kernel,
        "decode",
        [shape((STRIP, COLS, C), BF)],
        [pltpu.VMEM((STRIP + 4, PITCH, C), F32)],
        given=10,
        limit=8,
    )(strip, above, below, strip_p, above_p, below_p, conv_a, bias_a.reshape(1, C), conv_b, bias_b.reshape(1, C))
    return decoded, front


def solution(mesh):
    in_specs = (
        P("slab", None, "tile", None),
        P("slab", None, "tile"),
        P("slab", None, None),
        P("slab", None),
        P("slab", None, None),
        P("slab", None),
        P("slab", None),
        P("slab"),
        P(),
        P(),
        P(),
        P(),
    )
    out_specs = (P("slab", "tile", None), P("slab", None, "tile"))
    return jax.shard_map(body, mesh=mesh, in_specs=in_specs, out_specs=out_specs, check_vma=False)
```
